32 devices in a mesh: group: 4 (over y, x), dev: 8 (over z, core).
Axes of the slice: x: 2, y: 2, z: 4, core: 2. Of those that a mesh axis runs over, the one named last changes fastest.
Arguments:
- density: float32 [32, 320, 128], P(('group', 'dev')), may hold values from 0.5 to 2
- velocity: float32 [3, 32, 320, 128], P(None, ('group', 'dev')), may hold values from -0.75 to 0.75
- pressure: float32 [32, 320, 128], P(('group', 'dev')), may hold values from 0.5 to 2
- rbf_blocks: bfloat16 [2048, 128, 128], P(('group', 'dev')), may hold values from -0.5 to 0.5
- correlation: int32 [2048, 128], P(('group', 'dev')), may hold values from 0 to 319
- normals: float32 [2048, 3, 128], P(('group', 'dev')), may hold values from -6 to 6
- routes: int32 [2048, 1], P(('group', 'dev')), may hold values from 0 to 31; in each aligned block of 64 rows (0 to 63, 64 to 127, ...) at most 4 rows name the same one
- targets: int32 [2048], P(('group', 'dev')), may hold values from 0 to 31
- stiffness: bfloat16 [1024, 128, 128], P(('group', 'dev')), may hold values from -0.35 to 2.35
- coupling: bfloat16 [1024, 128, 128], P(('group', 'dev')), may hold values from -0.5 to 0.5
- inverse_diag: float32 [1024, 3, 128], P(('group', 'dev')), may hold values from 0.5 to 1.5
- displacement: float32 [1024, 3, 128], P(('group', 'dev')), may hold values from -6 to 6
- diff_res: float32 [8, 1024, 3, 128], P(None, ('group', 'dev')), may hold values from -2 to 2
- diff_disp: float32 [8, 1024, 3, 128], P(None, ('group', 'dev')), may hold values from -2.4 to 2.4
Outputs:
- fluid_next: float32 [5, 32, 320, 128], P(None, ('group', 'dev'))
- disp_next: float32 [1024, 3, 128], P(('group', 'dev'))
- wall_motion: float32 [2048, 3, 128], P(('group', 'dev'))
The draws below stay inside these ranges and needn't reach their ends.
Inputs may be any that keep to these rules, and one draw needn't show every extreme that they name: `routes`: among the 64 blocks of one device at most 4 name the same owner, and some device names one owner exactly 4 times.
All inputs are finite; a program needn't handle non-finite values.
Results may differ from the reference program's by a relative error of at most 0.0004.
The reference program's roundings to bfloat16 on the way (of `weighted` and `disp_half`) count: a program that leaves them out, or rounds other values in their place, can miss the bound.
Values may be sent and summed in bfloat16 or wider, within the bound.
A program may use at most 64 MiB of HBM per device.

```python
import math
import jax
import jax.numpy as jnp
import numpy as np
from jax import lax

CX = 1
CY = 320
CZ = 128
NB = 64
NS = 32
NODES = 128
M = 8
CAP = 4
NX = 32
NBT = 2048
NST = 1024
DEVICES = 32


def newton_parts(key):
    subkeys = jax.random.split(jax.random.fold_in(key, 4099), 7)
    position = (jnp.arange(NST, dtype=jnp.float32) / NST)[None, :, None, None]
    extent = (M, NST, 3, NODES)
    spread = 0.15 * jnp.power(3.0, position)
    private = jnp.clip(jax.random.normal(subkeys[0], extent, jnp.float32), -4.0, 4.0)
    shared = jnp.clip(jax.random.normal(subkeys[1], (1, NST, 3, NODES), jnp.float32), -4.0, 4.0)
    columns = spread * (private + 0.5 * shared)
    resting = 0.5 * jnp.clip(jax.random.normal(subkeys[2], (NST, 3, NODES), jnp.float32), -4.0, 4.0)
    columns = jnp.clip(columns, -2.0, 2.0)
    lead_signs = jnp.where(jax.random.bernoulli(subkeys[3], 0.5, (M,)), 1.0, -1.0)
    growth_signs = jnp.where(jax.random.bernoulli(subkeys[4], 0.5, (M,)), 1.0, -1.0)
    leading = lead_signs * jax.random.uniform(subkeys[5], (M,), jnp.float32, 0.3, 0.8)
    growth = growth_signs * jax.random.uniform(subkeys[6], (M,), jnp.float32, 0.4, 0.8)
    weights = leading[:, None, None, None] + growth[:, None, None, None] * position
    settled = jnp.clip(resting + jnp.sum(weights * columns, axis=0), -6.0, 6.0)
    return (columns, settled)


def draw_diff_res(key, part):
    return newton_parts(key)[0]


def draw_displacement(key, part):
    return newton_parts(key)[1]


def draw_stiffness(key, part):
    noise_key = jax.random.fold_in(key, 8191)
    offdiag = jnp.clip(jax.random.normal(noise_key, (NST, NODES, NODES), jnp.float32) / math.sqrt(NODES), -0.35, 0.35)
    return (2.0 * jnp.eye(NODES, dtype=jnp.float32)[None] + offdiag).astype(jnp.bfloat16)


def plant(result, own_key, low, top_value):
    index_at = [jax.random.randint(jax.random.fold_in(own_key, axis), (), 0, length) for axis, length in enumerate(result.shape)]
    longest = result.shape.index(max(result.shape))
    neighbour = index_at[:longest] + [(index_at[longest] + 1) % result.shape[longest]] + index_at[longest + 1:]
    return result.at[tuple(index_at)].set(low).at[tuple(neighbour)].set(top_value)


def block_scale(key, dims, cuts, least, top_value):
    level = 1.0
    for dim, blocks in cuts:
        heights = jax.random.uniform(jax.random.fold_in(jax.random.fold_in(key, 6), dim), (blocks,), jnp.float32, least / len(cuts), top_value / len(cuts))
        level = level * jnp.repeat(jnp.exp(heights), dims[dim] // blocks).reshape((-1,) + (1,) * (len(dims) - 1 - dim))
    return level


def routed_block(stream_key, own, number, rows, amount, top, bound, lean):
    ranking = jax.random.permutation(stream_key, amount)
    packed, ordinary = shares(amount, rows * top, bound, lean, True), shares(amount, rows * top, bound, lean, False)
    places = jnp.arange(amount)

    def named(sizes, offset_by):
        used = int((sizes > 0).sum())
        fixed = max(1, used // 4)
        passed = fixed + (places - fixed + offset_by * (used - fixed)) % max(1, amount - fixed)
        return jnp.zeros((amount,), jnp.int32).at[ranking[jnp.where(places < fixed, places, passed)]].set(jnp.asarray(sizes, jnp.int32))

    sizes = jnp.where(number % 4 == 0, named(packed, number // 4), named(ordinary, number - number // 4 - 1))
    mixed = jax.random.permutation(jax.random.fold_in(own, 3), amount)
    donor, sink = mixed[0:amount // 2 * 2:2], mixed[1:amount // 2 * 2:2]
    room = jnp.minimum(sizes[donor] - 1, bound - sizes[sink]) // 2
    room = jnp.where((donor == ranking[0]) | (sink == ranking[0]) | (sizes[sink] == 0), 0, jnp.maximum(room, 0))
    passed = jax.random.randint(jax.random.fold_in(own, 4), (amount // 2,), 0, 1 << 20) % (room + 1)
    sizes = sizes.at[donor].add(-passed).at[sink].add(passed)
    labels = jnp.searchsorted(jnp.cumsum(sizes), jnp.arange(rows * top), side="right").astype(jnp.int32)
    grid = labels.reshape(top, rows).T
    grid = grid[jax.random.permutation(jax.random.fold_in(own, 1), rows)]
    offset_by = jax.random.randint(jax.random.fold_in(own, 2), (rows, 1), 0, top)
    return jnp.take_along_axis(grid, (jnp.arange(top)[None, :] + offset_by) % top, axis=1)


def shares(count, total, most, skew, full):
    loads = [(1 << 20) // math.isqrt(rank ** skew) + 1 for rank in range(1, count + 1)]
    largest = most if full else min(most, max(-(-total // count), total * loads[0] // sum(loads)))
    least = 1 if total - largest >= count - 1 else 0
    counts, spare = [largest] + [least] * (count - 1), total - largest - least * (count - 1)
    while spare > 0:
        movable = [i for i in range(1, count) if counts[i] < largest] or [i for i in range(1, count) if counts[i] < most]
        whole, left = sum([loads[i] for i in movable]), spare
        for i in movable:
            addition = min(most - counts[i], max(1, left * loads[i] // whole), spare)
            counts[i] = counts[i] + addition
            spare = spare - addition
    return np.array(counts)


def gaussian(key, shape, width, most, pieces=(), kind=jnp.bfloat16):
    entries = width * jax.random.normal(key, shape, jnp.float32)
    if pieces:
        entries = entries * block_scale(key, shape, pieces, -0.22, 0.18)
    return jnp.clip(entries, -most, most).astype(kind)


def setup_inputs(seed: int = 0) -> dict:
    key_list = jax.random.split(jax.random.key(seed), 15)
    density = jnp.clip(jnp.exp(math.log(2.0) - 1.3862944 * jax.random.uniform(key_list[0], (NX, CY, CZ), jnp.float32) ** block_scale(key_list[0], (NX, CY, CZ), ((0, 32),), -0.2, 0.2)), 0.5, 2.0)
    velocity = gaussian(key_list[1], (3, NX, CY, CZ), 0.3, 0.75, ((1, 32),), jnp.float32)
    pressure = jnp.clip(jnp.exp(math.log(2.0) - 1.3862944 * jax.random.uniform(key_list[2], (NX, CY, CZ), jnp.float32) ** block_scale(key_list[2], (NX, CY, CZ), ((0, 32),), -0.2, 0.2)), 0.5, 2.0)
    rbf_blocks = gaussian(key_list[3], (NBT, NODES, NODES), NODES ** -0.5, 0.5, ((0, 32),))
    correlation = plant(jax.random.randint(key_list[4], (NBT, NODES), 0, CX * CY), jax.random.fold_in(key_list[4], 1), 0, (CX * CY) - 1).astype(jnp.int32)
    normals = gaussian(key_list[5], (NBT, 3, NODES), 1.0, 6.0, ((0, 32),), jnp.float32)
    routes_keys = jax.random.split(jax.random.fold_in(key_list[6], 1), NBT // NB)
    routes_turns = jax.random.permutation(jax.random.fold_in(key_list[6], 3), NBT // NB)
    routes = jax.vmap(lambda own, number: routed_block(jax.random.fold_in(key_list[6], 2), own, number, NB, DEVICES, 1, CAP, 2))(routes_keys, routes_turns).reshape((NBT, 1))
    targets = plant(jax.random.randint(key_list[7], (NBT,), 0, NS), jax.random.fold_in(key_list[7], 1), 0, NS - 1).astype(jnp.int32)
    stiffness = draw_stiffness(jax.random.fold_in(key_list[14], 71), 0)
    coupling = gaussian(key_list[9], (NST, NODES, NODES), NODES ** -0.5, 0.5, ((0, 32),))
    inverse_diag = jnp.clip(1.0 + 0.1 * jax.random.normal(key_list[10], (NST, 3, NODES), jnp.float32), 0.5, 1.5)
    displacement = draw_displacement(jax.random.fold_in(key_list[14], 71), 0)
    diff_res = draw_diff_res(jax.random.fold_in(key_list[14], 71), 0)
    diff_disp = gaussian(key_list[13], (M, NST, 3, NODES), 0.4, 2.4, ((1, 32),), jnp.float32)
    return {"density": density, "velocity": velocity, "pressure": pressure, "rbf_blocks": rbf_blocks, "correlation": correlation, "normals": normals, "routes": routes, "targets": targets, "stiffness": stiffness, "coupling": coupling, "inverse_diag": inverse_diag, "displacement": displacement, "diff_res": diff_res, "diff_disp": diff_disp}


ratio_heat = 1.4
step_ratio = 0.03

def euler_flux(state, normal_axis):
    dens = state[0]
    vel = state[1:4] / dens
    press = (ratio_heat - 1.0) * (state[4] - 0.5 * dens * lax.optimization_barrier(jnp.sum(vel * vel, axis=0)))
    normal_speed = vel[normal_axis]
    rows = [dens * normal_speed]
    for comp in range(3):
        moment = state[1 + comp] * normal_speed
        if comp == normal_axis:
            moment = moment + press
        rows.append(moment)
    rows.append((state[4] + press) * normal_speed)
    wave_speed = jnp.abs(normal_speed) + jnp.sqrt(ratio_heat * press / dens)
    return (jnp.stack(rows, axis=0), wave_speed)

def rusanov(left_state, right_state, normal_axis):
    flux_left, speed_left = euler_flux(left_state, normal_axis)
    flux_right, speed_right = euler_flux(right_state, normal_axis)
    return 0.5 * (flux_left + flux_right) - 0.5 * jnp.maximum(speed_left, speed_right) * (right_state - left_state)

def conserve(density, velocity, pressure):
    energy = pressure / (ratio_heat - 1.0) + 0.5 * density * lax.optimization_barrier(jnp.sum(velocity * velocity, axis=0))
    return jnp.concatenate([density[None], density[None] * velocity, energy[None]], axis=0)

def advance(padded, conserved):
    face_x = rusanov(padded[:, :-1], padded[:, 1:], 0)
    divergence = face_x[:, 1:] - face_x[:, :-1]
    face_y = rusanov(conserved, jnp.roll(conserved, -1, axis=2), 1)
    divergence = divergence + face_y - jnp.roll(face_y, 1, axis=2)
    mirror_sign = jnp.array([1.0, 1.0, 1.0, -1.0, 1.0], dtype=conserved.dtype)[:, None, None, None]
    padded_z = jnp.concatenate([conserved[..., :1] * mirror_sign, conserved, conserved[..., -1:]], axis=3)
    face_z = rusanov(padded_z[..., :-1], padded_z[..., 1:], 2)
    divergence = divergence + face_z[..., 1:] - face_z[..., :-1]
    return conserved - step_ratio * divergence

def wall_pressure(state):
    bottom = state[..., 0]
    return (ratio_heat - 1.0) * (bottom[4] - 0.5 * lax.optimization_barrier(jnp.sum(bottom[1:4] * bottom[1:4], axis=0)) / bottom[0])

def cho_apply(gram, projected):
    factor = jnp.linalg.cholesky(gram)
    middle = lax.linalg.triangular_solve(factor, projected[:, None], left_side=True, lower=True)
    return lax.linalg.triangular_solve(factor, middle, left_side=True, lower=True, transpose_a=True)[:, 0]

def reference(density, velocity, pressure, rbf_blocks, correlation, normals, routes, targets, stiffness, coupling, inverse_diag, displacement, diff_res, diff_disp):
    row_offsets = jnp.arange(CX + 2, dtype=jnp.int32)

    def slab_step(index, carry):
        fluid_all, wall_all = carry
        slab_index = jnp.asarray(index).astype(jnp.int32)
        start = (slab_index * CX).astype(jnp.int32)
        row_ids = ((start - 1 + row_offsets) % NX).astype(jnp.int32)
        piece = conserve(jnp.take(density, row_ids, axis=0), jnp.take(velocity, row_ids, axis=1), jnp.take(pressure, row_ids, axis=0))
        slab = advance(piece, piece[:, 1:-1])
        fluid_all = lax.dynamic_update_slice_in_dim(fluid_all, slab, start, 1)
        wall_all = lax.dynamic_update_slice_in_dim(wall_all, wall_pressure(slab).reshape(1, CX * CY), slab_index, 0)
        return (fluid_all, wall_all)
    fluid_start = jnp.zeros((5, NX, CY, CZ), jnp.float32)
    wall_start = jnp.zeros((DEVICES, CX * CY), jnp.float32)
    fluid_next, wall_rows = lax.fori_loop(0, DEVICES, slab_step, (fluid_start, wall_start))

    def map_loads(element):
        wall_row, indices, normal_rows, kernels = element
        weighted = (wall_row[indices][:, None, :] * normal_rows).astype(jnp.bfloat16)
        return jnp.einsum('bci,bij->bcj', weighted.astype(jnp.float32), kernels.astype(jnp.float32))
    block_load = lax.map(map_loads, (wall_rows, correlation.reshape(DEVICES, NB, NODES), normals.reshape(DEVICES, NB, 3, NODES), rbf_blocks.reshape(DEVICES, NB, NODES, NODES)))
    block_load = block_load.reshape(NBT, 3, NODES)
    solid_ids = (routes[:, 0] * NS + targets).astype(jnp.int32)
    solid_load = jax.ops.segment_sum(block_load, solid_ids, num_segments=NST)
    disp_half = displacement.astype(jnp.bfloat16)
    earlier = jnp.concatenate([jnp.zeros((1, 3, NODES), jnp.bfloat16), disp_half[:-1]], axis=0)
    solid_res = jnp.einsum('bcj,bij->bci', disp_half.astype(jnp.float32), stiffness.astype(jnp.float32))
    solid_res = solid_res + jnp.einsum('bcj,bij->bci', earlier.astype(jnp.float32), coupling.astype(jnp.float32)) - solid_load
    coupling_res = -inverse_diag * solid_res
    gram = jnp.einsum('mbcj,nbcj->mn', diff_res, diff_res, precision=lax.Precision.HIGHEST)
    projected = jnp.einsum('mbcj,bcj->m', diff_res, coupling_res, precision=lax.Precision.HIGHEST)
    mixing = -cho_apply(gram, projected)
    disp_next = displacement + coupling_res + jnp.einsum('mbcj,m->bcj', diff_disp, mixing, precision=lax.Precision.HIGHEST)
    reply = disp_next.astype(jnp.bfloat16)[solid_ids]

    def map_motion(element):
        kernels, rows = element
        return jnp.einsum('bij,bcj->bci', kernels.astype(jnp.float32), rows.astype(jnp.float32))
    wall_motion = lax.map(map_motion, (rbf_blocks.reshape(DEVICES, NB, NODES, NODES), reply.reshape(DEVICES, NB, 3, NODES)))
    return (fluid_next, disp_next, wall_motion.reshape(NBT, 3, NODES))
```

```python
import functools

import jax
import jax.numpy as jnp
from jax import lax
from jax.experimental import pallas as pl
from jax.experimental.pallas import tpu as pltpu
from jax.sharding import PartitionSpec as P

ratio_heat = 1.4
step_ratio = 0.03
AXES = ("group", "dev")
LOGICAL = pl.DeviceIdType.LOGICAL
LAST = (((1,), (1,)), ((), ()))
WIDE = 12


def conserve(prim):
    dens, u, v, w, press = prim
    energy = press / (ratio_heat - 1.0) + 0.5 * dens * (u * u + v * v + w * w)
    return (dens, dens * u, dens * v, dens * w, energy)


def flux_parts(prim, axis):
    state = conserve(prim)
    normal = prim[1 + axis]
    press = prim[4]
    rows = [row * normal for row in state]
    rows[1 + axis] = rows[1 + axis] + press
    rows[4] = rows[4] + press * normal
    speed = jnp.abs(normal) + jnp.sqrt(ratio_heat * press / prim[0])
    return state, rows, speed


def face_difference(low, mid, high, axis):
    state_l, flux_l, speed_l = flux_parts(low, axis)
    state_m, _, speed_m = flux_parts(mid, axis)
    state_h, flux_h, speed_h = flux_parts(high, axis)
    upper = jnp.maximum(speed_m, speed_h)
    lower = jnp.maximum(speed_l, speed_m)
    return [
        0.5 * (fh - fl) - 0.5 * (upper * (sh - sm) - lower * (sm - sl))
        for fh, fl, sh, sm, sl in zip(flux_h, flux_l, state_h, state_m, state_l)
    ]


def advance(mid, x_pair, y_pair, z_pair):
    div_x = face_difference(x_pair[0], mid, x_pair[1], 0)
    div_y = face_difference(y_pair[0], mid, y_pair[1], 1)
    div_z = face_difference(z_pair[0], mid, z_pair[1], 2)
    return [
        row - step_ratio * (a + b + c)
        for row, a, b, c in zip(conserve(mid), div_x, div_y, div_z)
    ]


def flow_section(fields, low_ref, high_ref, out_ref):
    height, lanes = fields[0].shape
    chunk = next(c for c in (32, 16, 8, height) if height % c == 0)
    row = lax.broadcasted_iota(jnp.int32, (chunk, lanes), 0)
    lane = lax.broadcasted_iota(jnp.int32, (chunk, lanes), 1)
    for start in range(0, height, chunk):
        rows = slice(start, start + chunk)
        before = (start - 1) % height
        after = (start + chunk) % height
        mid = [f[rows, :] for f in fields]
        y_low = [
            jnp.where(row == 0, f[before : before + 1, :], pltpu.roll(m, 1, 0))
            for f, m in zip(fields, mid)
        ]
        y_high = [
            jnp.where(row == chunk - 1, f[after : after + 1, :], pltpu.roll(m, chunk - 1, 0))
            for f, m in zip(fields, mid)
        ]
        signs = (1.0, 1.0, 1.0, -1.0, 1.0)
        z_low = [jnp.where(lane == 0, s * m, pltpu.roll(m, 1, 1)) for s, m in zip(signs, mid)]
        z_high = [jnp.where(lane == lanes - 1, m, pltpu.roll(m, lanes - 1, 1)) for m in mid]
        x_low = [low_ref[i, rows, :].astype(jnp.float32) for i in range(5)]
        x_high = [high_ref[i, rows, :].astype(jnp.float32) for i in range(5)]
        result = advance(mid, (x_low, x_high), (y_low, y_high), (z_low, z_high))
        for i in range(5):
            out_ref[i, 0, rows, :] = result[i]


def thirds(value):
    high = value.astype(jnp.bfloat16)
    rest = value - high.astype(jnp.float32)
    middle = rest.astype(jnp.bfloat16)
    low = (rest - middle.astype(jnp.float32)).astype(jnp.bfloat16)
    return high, middle, low


def couple_kernel(
    peers,
    width,
    dens_hbm,
    vel_hbm,
    press_hbm,
    owner_hbm,
    target_hbm,
    res_hbm,
    disp_hbm,
    index_hbm,
    normals_hbm,
    rbf_hbm,
    stiff_hbm,
    coup_hbm,
    inv_hbm,
    dif_hbm,
    fluid_ref,
    next_ref,
    motion_ref,
    dens_ref,
    vel_ref,
    press_ref,
    owner_ref,
    target_ref,
    res_ref,
    disp_ref,
    index_ref,
    normals_ref,
    rbf_ref,
    stiff_ref,
    coup_ref,
    inv_ref,
    dif_ref,
    ends,
    prim,
    low_ref,
    high_ref,
    side_ref,
    prior_ref,
    note_out,
    note_in,
    load_out,
    load_in,
    reply_out,
    reply_in,
    stat_out,
    stat_in,
    pick,
    place3,
    lanes_in,
    lanes_out,
    slots,
    held,
    solid,
    lines,
    fetch_sem,
    near_send,
    near_recv,
    note_sem,
    load_sem,
    stat_sem,
    reply_sem,
):
    f32, bf16 = jnp.float32, jnp.bfloat16
    me = lax.axis_index("group") * width + lax.axis_index("dev")
    blocks, nodes = index_ref.shape
    count = disp_ref.shape[1]
    columns = res_ref.shape[0]
    capacity = load_out.shape[1]
    slot_count = peers * capacity
    height, depth = dens_ref.shape[1:]
    tail = prior_ref.shape[1]
    spans = [slice(c * nodes, (c + 1) * nodes) for c in range(3)]
    half = peers // 2
    steps = sorted(range(1, peers), key=lambda d: abs(d - half))

    def hop(distance):
        return lax.rem(me + distance, peers)

    fetches = {}

    def fetch(name, src, dst):
        copy = pltpu.make_async_copy(src, dst, fetch_sem.at[len(fetches)])
        copy.start()
        fetches[name] = copy

    fetch("dens", dens_hbm, dens_ref)
    fetch("vel", vel_hbm, vel_ref)
    fetch("press", press_hbm, press_ref)
    barrier = pltpu.get_barrier_semaphore()
    for step in steps:
        pl.semaphore_signal(barrier, inc=1, device_id=hop(step), device_id_type=LOGICAL)
    fetch("owner", owner_hbm, owner_ref)
    fetch("target", target_hbm, target_ref)
    fetch("disp", disp_hbm, disp_ref)
    fetch("res", res_hbm, res_ref)
    fetch("index", index_hbm, index_ref)
    fetch("normals", normals_hbm, normals_ref)
    fetch("stiff", stiff_hbm, stiff_ref)
    fetch("coup", coup_hbm, coup_ref)
    fetch("rbf", rbf_hbm, rbf_ref)
    fetch("inv", inv_hbm, inv_ref)
    fetch("dif", dif_hbm, dif_ref)

    lanes_in[...] = jnp.zeros_like(lanes_in)
    held[...] = jnp.zeros_like(held)
    ends[...] = jnp.ones_like(ends)

    fetches["dens"].wait()
    fetches["vel"].wait()
    fetches["press"].wait()
    fields = [dens_ref.at[0]] + [vel_ref.at[i, 0] for i in range(3)] + [press_ref.at[0]]
    for i, field in enumerate(fields):
        for start in range(0, height, depth):
            part = field[start : min(start + depth, height), :]
            if part.shape[0] < depth:
                part = jnp.concatenate(
                    [part, jnp.ones((depth - part.shape[0], depth), f32)], axis=0
                )
            turned = part.T
            for z in range(2):
                ends[z, i : i + 1, start : start + depth] = turned[z : z + 1, :]
    for i, field in enumerate(fields):
        prim[i] = field[...].astype(bf16)

    edge = ends[0]
    total = edge.shape[1]
    lane = lax.broadcasted_iota(jnp.int32, edge.shape, 1)
    ahead = jnp.where(lane == height - 1, edge[:, 0:1], pltpu.roll(edge, total - 1, 1))
    behind = jnp.where(lane == 0, edge[:, height - 1 : height], pltpu.roll(edge, 1, 1))
    ends[2] = ahead
    ends[3] = behind

    def variant(ref, i):
        return [ref[i, k : k + 1, :] for k in range(5)]

    mid = variant(ends, 0)
    mirror = list(mid)
    mirror[3] = -mirror[3]
    div_y = face_difference(variant(ends, 3), mid, variant(ends, 2), 1)
    div_z = face_difference(mirror, mid, variant(ends, 1), 2)
    for i in range(5):
        ends[2, i : i + 1, :] = div_y[i] + div_z[i]

    fetches["owner"].wait()
    fetches["target"].wait()
    owner_row = owner_ref[...].astype(f32)
    target_row = target_ref[...].astype(f32)
    row_id = lax.broadcasted_iota(jnp.int32, (blocks, blocks), 0)
    column_id = lax.broadcasted_iota(jnp.int32, (blocks, blocks), 1)
    diagonal = row_id == column_id
    owner = jnp.sum(jnp.where(diagonal, owner_row, 0.0), axis=1, keepdims=True)
    target = jnp.sum(jnp.where(diagonal, target_row, 0.0), axis=1, keepdims=True)
    same = jnp.where(owner == owner_row, 1.0, 0.0)
    rank = jnp.sum(jnp.where(column_id < row_id, same, 0.0), axis=1, keepdims=True)
    rank_row = jnp.sum(jnp.where(row_id < column_id, same, 0.0), axis=0, keepdims=True)
    lane_id = lax.broadcasted_iota(jnp.int32, (blocks, slot_count), 1).astype(f32)
    pick[...] = jnp.where(owner * capacity + rank == lane_id, 1.0, 0.0).astype(bf16)
    line_id = lax.broadcasted_iota(jnp.int32, (slot_count, blocks), 0).astype(f32)
    placed = jnp.where(owner_row * capacity + rank_row == line_id, 1.0, 0.0).astype(bf16)
    for part in range(3):
        place3[:, part * blocks : (part + 1) * blocks] = placed
    mine = (me * capacity).astype(f32)
    marks = jnp.where(mine + rank == lane_id, target + 1.0, 0.0).astype(bf16)
    peer_id = lax.broadcasted_iota(jnp.int32, (peers, blocks), 0).astype(f32)
    owned = jnp.where(peer_id == owner_row, 1.0, 0.0).astype(bf16)
    tags = jnp.dot(owned, marks, preferred_element_type=f32)
    for p in range(peers):
        note_out[p, :, 0:slot_count] = tags[p : p + 1, :]

    fetches["disp"].wait()
    pl.semaphore_wait(barrier, peers - 1)

    def near(slot, src, dst, distance):
        return pltpu.make_async_remote_copy(
            src_ref=src,
            dst_ref=dst,
            send_sem=near_send.at[slot],
            recv_sem=near_recv.at[slot],
            device_id=hop(distance),
            device_id_type=LOGICAL,
        )

    wall_up = near(0, ends.at[0], side_ref.at[0], 1)
    wall_down = near(1, ends.at[0], side_ref.at[1], peers - 1)
    prior = near(2, disp_ref.at[:, pl.ds(count - tail, tail), :], prior_ref, 1)
    early, late = pl.ds(0, 3), pl.ds(3, 2)
    bulk_early = (
        near(3, prim.at[early], low_ref.at[early], 1),
        near(4, prim.at[early], high_ref.at[early], peers - 1),
    )
    bulk_late = (
        near(5, prim.at[late], low_ref.at[late], 1),
        near(6, prim.at[late], high_ref.at[late], peers - 1),
    )

    def spread(src, dst, sem, indexed):
        for step in steps:
            peer = hop(step)
            pltpu.make_async_remote_copy(
                src_ref=src.at[peer] if indexed else src,
                dst_ref=dst.at[me],
                send_sem=sem.at[0],
                recv_sem=sem.at[1],
                device_id=peer,
                device_id_type=LOGICAL,
            ).start()

    def gather(dst, sem):
        whole = dst.at[pl.ds(0, peers - 1)]
        return pltpu.make_async_remote_copy(
            src_ref=whole,
            dst_ref=whole,
            send_sem=sem.at[0],
            recv_sem=sem.at[1],
            device_id=hop(1),
            device_id_type=LOGICAL,
        )

    wall_up.start()
    wall_down.start()
    prior.start()

    fetches["res"].wait()
    for m in range(columns):
        for n in range(m, columns):
            line = jnp.sum(jnp.sum(res_ref[m] * res_ref[n], axis=0), axis=0, keepdims=True)
            lines[m * columns + n : m * columns + n + 1, :] = line
            lines[n * columns + m : n * columns + m + 1, :] = line

    def turn(value):
        kept = jnp.sum(value, axis=1, keepdims=True)
        shape = (value.shape[0], nodes)
        at = lax.broadcasted_iota(jnp.int32, shape, 0) == lax.broadcasted_iota(jnp.int32, shape, 1)
        return jnp.sum(jnp.where(at, kept, 0.0), axis=0, keepdims=True)

    gram_row = turn(lines[...])
    for p in range(peers):
        note_out[p, :, slot_count : slot_count + nodes] = gram_row
    spread(note_out, note_in, note_sem, True)
    for copy in bulk_early:
        copy.start()
    note_in[me] = note_out[me]

    for c in range(3):
        held[pl.ds(8 + c, count, stride=8), :] = disp_ref[c]
    fetches["stiff"].wait()
    fetches["coup"].wait()

    def residual(t):
        both = jnp.concatenate([held[8 * t + 8 : 8 * t + 16, :], held[8 * t : 8 * t + 8, :]], axis=1)
        weights = jnp.concatenate([stiff_ref[t], coup_ref[t]], axis=1)
        solid[8 * t : 8 * t + 8, :] = lax.dot_general(
            both.astype(bf16), weights, LAST, preferred_element_type=f32
        )

    for t in range(1, count):
        residual(t)

    fetches["index"].wait()
    fetches["normals"].wait()
    fetches["rbf"].wait()
    wall_up.wait()
    wall_down.wait()

    div_x = face_difference(variant(side_ref, 0), mid, variant(side_ref, 1), 0)
    bottom = [
        row - step_ratio * (a + ends[2, i : i + 1, :])
        for i, (row, a) in enumerate(zip(conserve(mid), div_x))
    ]
    kinetic = bottom[1] * bottom[1] + bottom[2] * bottom[2] + bottom[3] * bottom[3]
    wall = (ratio_heat - 1.0) * (bottom[4] - 0.5 * kinetic / bottom[0])

    index = index_ref[...]
    low = index % nodes
    found = jnp.zeros(index.shape, f32)
    for part in range(wall.shape[1] // nodes):
        source = jnp.broadcast_to(wall[:, part * nodes : (part + 1) * nodes], index.shape)
        taken = jnp.take_along_axis(source, low, axis=1)
        found = jnp.where(index // nodes == part, taken, found)
    for c in range(3):
        lanes_in[pl.ds(c, blocks, stride=WIDE), :] = found * normals_ref[c]

    def pair(b):
        at = WIDE * b
        return jnp.concatenate(
            [lanes_in[at : at + 8, :], lanes_in[at + 8 : at + 16, :]], axis=1
        ).astype(bf16)

    for b in range(0, blocks, 2):
        weights = rbf_ref[b : b + 2].reshape(2 * nodes, nodes)
        lanes_out[4 * b : 4 * b + 8, :] = jnp.dot(pair(b), weights, preferred_element_type=f32)
    parts = [thirds(lanes_out[pl.ds(c, blocks, stride=4), :]) for c in range(3)]
    for c in range(3):
        stack = jnp.concatenate(parts[c], axis=0)
        placed = jnp.dot(place3[...], stack, preferred_element_type=f32)
        for p in range(peers):
            load_out[p, :, spans[c]] = placed[p * capacity : (p + 1) * capacity, :]
    spread(load_out, load_in, load_sem, True)
    load_in[me] = load_out[me]

    prior.wait()
    first = (me > 0).astype(f32)
    for c in range(3):
        held[c : c + 1, :] = prior_ref[c, tail - 1 : tail, :] * first
    residual(0)

    notes = gather(note_in, note_sem)
    notes.wait_recv()
    note = jnp.sum(note_in[...], axis=0)
    tag_row = note[:, 0:slot_count]
    marked = lax.broadcasted_iota(jnp.int32, (nodes, slot_count), 0).astype(f32) + 1.0 == tag_row
    marked = jnp.where(marked, 1.0, 0.0)
    collector = marked[0:count, :].astype(bf16)
    chooser = marked.T[:, 0:count].astype(bf16)
    shape = (columns, nodes)
    m_id = lax.broadcasted_iota(jnp.int32, shape, 0)
    n_id = lax.broadcasted_iota(jnp.int32, shape, 1)
    spot = jnp.minimum(m_id * columns + n_id, nodes - 1)
    gram = jnp.broadcast_to(note[:, slot_count : slot_count + nodes], shape)
    matrix = jnp.where(
        n_id < columns,
        jnp.take_along_axis(gram, spot, axis=1),
        jnp.where(n_id == m_id + columns, 1.0, 0.0),
    )
    for k in range(columns):
        line = matrix[k : k + 1, :]
        scaled = line / matrix[k : k + 1, k : k + 1]
        matrix = jnp.where(m_id == k, scaled, matrix - matrix[:, k : k + 1] * scaled)
    fetches["inv"].wait()
    fetches["dif"].wait()

    loads = gather(load_in, load_sem)
    loads.wait_recv()
    for p in range(peers):
        slots[p * capacity : (p + 1) * capacity, :] = load_in[p]
    high, middle, rest = thirds(slots[...])
    twice = jnp.concatenate([collector, collector], axis=1)
    served = jnp.dot(
        twice, jnp.concatenate([high, middle], axis=0), preferred_element_type=f32
    ) + jnp.dot(collector, rest, preferred_element_type=f32)
    change = [
        -inv_ref[c] * (solid[pl.ds(c, count, stride=8), :] - served[:, spans[c]])
        for c in range(3)
    ]
    for m in range(columns):
        line = sum(res_ref[m, c] * change[c] for c in range(3))
        lines[m : m + 1, :] = jnp.sum(line, axis=0, keepdims=True)
    share = sum(
        -matrix[:, columns + m : columns + m + 1] * lines[m : m + 1, :] for m in range(columns)
    )
    stat_out[...] = turn(share)
    spread(stat_out, stat_in, stat_sem, False)
    for copy in bulk_late:
        copy.start()
    stat_in[me] = stat_out[...]
    base = [disp_ref[c] + change[c] for c in range(3)]
    stats = gather(stat_in, stat_sem)
    stats.wait_recv()
    mixing = jnp.broadcast_to(jnp.sum(stat_in[...], axis=0), (8, nodes))
    weights = [
        jnp.tile(jnp.broadcast_to(mixing[:, m : m + 1], (8, nodes)), (count // 8, 1))
        for m in range(columns)
    ]
    halves = []
    for c in range(3):
        result = base[c]
        for m in range(columns):
            result = result + dif_ref[m, c] * weights[m]
        next_ref[c] = result
        halves.append(result.astype(bf16))
    chosen = jnp.dot(chooser, jnp.concatenate(halves, axis=1), preferred_element_type=f32)
    for p in range(peers):
        reply_out[p] = chosen[p * capacity : (p + 1) * capacity, :].astype(bf16)
    spread(reply_out, reply_in, reply_sem, True)
    reply_in[me] = reply_out[me]

    for copy in bulk_early + bulk_late:
        copy.wait()
    flow_section(fields, low_ref, high_ref, fluid_ref)

    replies = gather(reply_in, reply_sem)
    replies.wait_recv()
    for p in range(peers):
        slots[p * capacity : (p + 1) * capacity, :] = reply_in[p].astype(f32)
    rows = jnp.dot(pick[...], slots[...].astype(bf16), preferred_element_type=f32)
    for c in range(3):
        lanes_in[pl.ds(c, blocks, stride=WIDE), :] = rows[:, spans[c]]
    for b in range(0, blocks, 2):
        weights = jnp.concatenate([rbf_ref[b], rbf_ref[b + 1]], axis=1)
        lanes_out[4 * b : 4 * b + 8, :] = lax.dot_general(
            pair(b), weights, LAST, preferred_element_type=f32
        )
    for c in range(3):
        motion_ref[c] = lanes_out[pl.ds(c, blocks, stride=4), :]
    for copy in (notes, loads, stats, replies):
        copy.wait_send()


def finish_kernel(fluid_in, next_in, motion_in, fluid_ref, next_ref, motion_ref, sems):
    pairs = ((fluid_in, fluid_ref), (next_in, next_ref), (motion_in, motion_ref))
    copies = [pltpu.make_async_copy(a, b, sems.at[i]) for i, (a, b) in enumerate(pairs)]
    for copy in copies:
        copy.start()
    for copy in copies:
        copy.wait()


def rows_last(value):
    return jnp.swapaxes(value, -3, -2)


def on_device(
    density,
    velocity,
    pressure,
    rbf_blocks,
    correlation,
    normals,
    routes,
    targets,
    stiffness,
    coupling,
    inverse_diag,
    displacement,
    diff_res,
    diff_disp,
):
    f32, bf16, i32 = jnp.float32, jnp.bfloat16, jnp.int32
    width = lax.axis_size("dev")
    peers = lax.axis_size(AXES)
    blocks, nodes = correlation.shape
    count = displacement.shape[0]
    columns = diff_res.shape[0]
    height, depth = density.shape[1:]
    capacity = max(2, 2 * blocks // peers)
    slot_count = peers * capacity
    row = 3 * nodes

    padded = -(-height // depth) * depth
    halo = (5, height, depth)
    vmem = pl.BlockSpec(memory_space=pltpu.VMEM)
    hbm = pl.BlockSpec(memory_space=pltpu.HBM)
    anywhere = pl.BlockSpec(memory_space=pl.ANY)
    dma = pltpu.SemaphoreType.DMA
    shapes = (
        jax.ShapeDtypeStruct((5,) + density.shape, f32),
        jax.ShapeDtypeStruct((3, count, nodes), f32),
        jax.ShapeDtypeStruct((3, blocks, nodes), f32),
    )
    operands = (
        density,
        velocity,
        pressure,
        routes.reshape(1, blocks),
        targets.reshape(1, blocks),
        rows_last(diff_res),
        rows_last(displacement),
        correlation,
        rows_last(normals),
        rbf_blocks,
        stiffness,
        coupling,
        rows_last(inverse_diag),
        rows_last(diff_disp),
    )
    operands = [pltpu.with_memory_space_constraint(x, pltpu.HBM) for x in operands]
    outputs = pl.pallas_call(
        functools.partial(couple_kernel, peers, width),
        out_shape=shapes,
        in_specs=[hbm] * len(operands),
        out_specs=(vmem, vmem, vmem),
        scratch_shapes=[pltpu.VMEM(x.shape, x.dtype) for x in operands]
        + [
            pltpu.VMEM((4, 8, padded), f32),
            pltpu.VMEM(halo, bf16),
            pltpu.VMEM(halo, bf16),
            pltpu.VMEM(halo, bf16),
            pltpu.VMEM((2, 8, padded), f32),
            pltpu.VMEM((3, 8, nodes), f32),
            pltpu.VMEM((peers, 1, slot_count + nodes), f32),
            pltpu.VMEM((peers, 1, slot_count + nodes), f32),
            pltpu.VMEM((peers, capacity, row), f32),
            pltpu.VMEM((peers, capacity, row), f32),
            pltpu.VMEM((peers, capacity, row), bf16),
            pltpu.VMEM((peers, capacity, row), bf16),
            pltpu.VMEM((1, nodes), f32),
            pltpu.VMEM((peers, 1, nodes), f32),
            pltpu.VMEM((blocks, slot_count), bf16),
            pltpu.VMEM((slot_count, 3 * blocks), bf16),
            pltpu.VMEM((blocks * WIDE, nodes), f32),
            pltpu.VMEM((blocks * 4, nodes), f32),
            pltpu.VMEM((slot_count, row), f32),
            pltpu.VMEM((count * 8 + 8, nodes), f32),
            pltpu.VMEM((count * 8, nodes), f32),
            pltpu.VMEM((columns * columns, nodes), f32),
            dma((len(operands),)),
            dma((7,)),
            dma((7,)),
            dma((2,)),
            dma((2,)),
            dma((2,)),
            dma((2,)),
        ],
        compiler_params=pltpu.CompilerParams(
            collective_id=0, has_side_effects=True, vmem_limit_bytes=24 * 2**20
        ),
    )(*operands)
    fluid_next, disp_next, wall_motion = pl.pallas_call(
        finish_kernel,
        out_shape=shapes,
        in_specs=[vmem] * 3,
        out_specs=(anywhere,) * 3,
        scratch_shapes=[dma((3,))],
        compiler_params=pltpu.CompilerParams(vmem_limit_bytes=16 * 2**20),
    )(*outputs)
    return (fluid_next, rows_last(disp_next), rows_last(wall_motion))


def solution(mesh):
    placed = (
        P(("group", "dev"), None, None),
        P(None, ("group", "dev"), None, None),
        P(("group", "dev"), None, None),
        P(("group", "dev"), None, None),
        P(("group", "dev"), None),
        P(("group", "dev"), None, None),
        P(("group", "dev"), None),
        P(("group", "dev")),
        P(("group", "dev"), None, None),
        P(("group", "dev"), None, None),
        P(("group", "dev"), None, None),
        P(("group", "dev"), None, None),
        P(None, ("group", "dev"), None, None),
        P(None, ("group", "dev"), None, None),
    )
    return jax.shard_map(
        on_device,
        mesh=mesh,
        in_specs=placed,
        out_specs=(
            P(None, ("group", "dev"), None, None),
            P(("group", "dev"), None, None),
            P(("group", "dev"), None, None),
        ),
        check_vma=False,
    )
```

```python
import functools

import jax
import jax.numpy as jnp
from jax import lax
from jax.experimental import pallas as pl
from jax.experimental.pallas import tpu as pltpu
from jax.sharding import PartitionSpec as P

ratio_heat = 1.4
step_ratio = 0.03
AXES = ("group", "dev")
LOGICAL = pl.DeviceIdType.LOGICAL
LAST = (((1,), (1,)), ((), ()))
WIDE = 12


def conserve(prim):
    dens, u, v, w, press = prim
    energy = press / (ratio_heat - 1.0) + 0.5 * dens * (u * u + v * v + w * w)
    return (dens, dens * u, dens * v, dens * w, energy)


def flux_parts(prim, axis):
    state = conserve(prim)
    normal = prim[1 + axis]
    press = prim[4]
    rows = [row * normal for row in state]
    rows[1 + axis] = rows[1 + axis] + press
    rows[4] = rows[4] + press * normal
    speed = jnp.abs(normal) + jnp.sqrt(ratio_heat * press / prim[0])
    return state, rows, speed


def face_difference(low, mid, high, axis):
    state_l, flux_l, speed_l = flux_parts(low, axis)
    state_m, _, speed_m = flux_parts(mid, axis)
    state_h, flux_h, speed_h = flux_parts(high, axis)
    upper = jnp.maximum(speed_m, speed_h)
    lower = jnp.maximum(speed_l, speed_m)
    return [
        0.5 * (fh - fl) - 0.5 * (upper * (sh - sm) - lower * (sm - sl))
        for fh, fl, sh, sm, sl in zip(flux_h, flux_l, state_h, state_m, state_l)
    ]


def advance(mid, x_pair, y_pair, z_pair):
    div_x = face_difference(x_pair[0], mid, x_pair[1], 0)
    div_y = face_difference(y_pair[0], mid, y_pair[1], 1)
    div_z = face_difference(z_pair[0], mid, z_pair[1], 2)
    return [
        row - step_ratio * (a + b + c)
        for row, a, b, c in zip(conserve(mid), div_x, div_y, div_z)
    ]


def flow_section(fields, low_ref, high_ref, out_ref):
    height, lanes = fields[0].shape
    chunk = next(c for c in (32, 16, 8, height) if height % c == 0)
    row = lax.broadcasted_iota(jnp.int32, (chunk, lanes), 0)
    lane = lax.broadcasted_iota(jnp.int32, (chunk, lanes), 1)
    for start in range(0, height, chunk):
        rows = slice(start, start + chunk)
        before = (start - 1) % height
        after = (start + chunk) % height
        mid = [f[rows, :] for f in fields]
        y_low = [
            jnp.where(row == 0, f[before : before + 1, :], pltpu.roll(m, 1, 0))
            for f, m in zip(fields, mid)
        ]
        y_high = [
            jnp.where(row == chunk - 1, f[after : after + 1, :], pltpu.roll(m, chunk - 1, 0))
            for f, m in zip(fields, mid)
        ]
        signs = (1.0, 1.0, 1.0, -1.0, 1.0)
        z_low = [jnp.where(lane == 0, s * m, pltpu.roll(m, 1, 1)) for s, m in zip(signs, mid)]
        z_high = [jnp.where(lane == lanes - 1, m, pltpu.roll(m, lanes - 1, 1)) for m in mid]
        x_low = [low_ref[i, rows, :].astype(jnp.float32) for i in range(5)]
        x_high = [high_ref[i, rows, :].astype(jnp.float32) for i in range(5)]
        result = advance(mid, (x_low, x_high), (y_low, y_high), (z_low, z_high))
        for i in range(5):
            out_ref[i, 0, rows, :] = result[i]


def thirds(value):
    high = value.astype(jnp.bfloat16)
    rest = value - high.astype(jnp.float32)
    middle = rest.astype(jnp.bfloat16)
    low = (rest - middle.astype(jnp.float32)).astype(jnp.bfloat16)
    return high, middle, low


def couple_kernel(
    peers,
    width,
    dens_hbm,
    vel_hbm,
    press_hbm,
    owner_hbm,
    target_hbm,
    res_hbm,
    disp_hbm,
    index_hbm,
    normals_hbm,
    rbf_hbm,
    stiff_hbm,
    coup_hbm,
    inv_hbm,
    dif_hbm,
    fluid_ref,
    next_ref,
    motion_ref,
    dens_ref,
    vel_ref,
    press_ref,
    owner_ref,
    target_ref,
    res_ref,
    disp_ref,
    index_ref,
    normals_ref,
    rbf_ref,
    stiff_ref,
    coup_ref,
    inv_ref,
    dif_ref,
    ends,
    prim,
    low_ref,
    high_ref,
    side_ref,
    prior_ref,
    note_out,
    note_in,
    load_out,
    load_in,
    reply_out,
    reply_in,
    stat_out,
    stat_in,
    pick,
    place3,
    lanes_in,
    lanes_out,
    slots,
    held,
    solid,
    lines,
    fetch_sem,
    near_send,
    near_recv,
    note_sem,
    load_sem,
    stat_sem,
    reply_sem,
):
    f32, bf16 = jnp.float32, jnp.bfloat16
    me = lax.axis_index("group") * width + lax.axis_index("dev")
    blocks, nodes = index_ref.shape
    count = disp_ref.shape[1]
    columns = res_ref.shape[0]
    capacity = load_out.shape[1]
    slot_count = peers * capacity
    height, depth = dens_ref.shape[1:]
    tail = prior_ref.shape[1]
    spans = [slice(c * nodes, (c + 1) * nodes) for c in range(3)]
    half = peers // 2
    steps = sorted(range(1, peers), key=lambda d: ((d % width) // 2 != width // 4, -(d % width), d))
    greeted = sorted(range(1, peers), key=lambda d: -abs(d - half))

    def hop(distance):
        return lax.rem(me + distance, peers)

    fetches = {}

    def fetch(name, src, dst):
        copy = pltpu.make_async_copy(src, dst, fetch_sem.at[len(fetches)])
        copy.start()
        fetches[name] = copy

    fetch("dens", dens_hbm, dens_ref)
    fetch("vel", vel_hbm, vel_ref)
    fetch("press", press_hbm, press_ref)
    barrier = pltpu.get_barrier_semaphore()
    for step in greeted:
        pl.semaphore_signal(barrier, inc=1, device_id=hop(step), device_id_type=LOGICAL)
    fetch("owner", owner_hbm, owner_ref)
    fetch("target", target_hbm, target_ref)
    fetch("disp", disp_hbm, disp_ref)
    fetch("res", res_hbm, res_ref)
    fetch("index", index_hbm, index_ref)
    fetch("normals", normals_hbm, normals_ref)
    fetch("stiff", stiff_hbm, stiff_ref)
    fetch("coup", coup_hbm, coup_ref)
    fetch("rbf", rbf_hbm, rbf_ref)
    fetch("inv", inv_hbm, inv_ref)
    fetch("dif", dif_hbm, dif_ref)

    lanes_in[...] = jnp.zeros_like(lanes_in)
    held[...] = jnp.zeros_like(held)
    ends[...] = jnp.ones_like(ends)

    fetches["dens"].wait()
    fetches["vel"].wait()
    fetches["press"].wait()
    fields = [dens_ref.at[0]] + [vel_ref.at[i, 0] for i in range(3)] + [press_ref.at[0]]
    for i, field in enumerate(fields):
        for start in range(0, height, depth):
            part = field[start : min(start + depth, height), :]
            if part.shape[0] < depth:
                part = jnp.concatenate(
                    [part, jnp.ones((depth - part.shape[0], depth), f32)], axis=0
                )
            turned = part.T
            for z in range(2):
                ends[z, i : i + 1, start : start + depth] = turned[z : z + 1, :]
    for i, field in enumerate(fields):
        prim[i] = field[...].astype(bf16)

    edge = ends[0]
    total = edge.shape[1]
    lane = lax.broadcasted_iota(jnp.int32, edge.shape, 1)
    ahead = jnp.where(lane == height - 1, edge[:, 0:1], pltpu.roll(edge, total - 1, 1))
    behind = jnp.where(lane == 0, edge[:, height - 1 : height], pltpu.roll(edge, 1, 1))
    ends[2] = ahead
    ends[3] = behind

    def variant(ref, i):
        return [ref[i, k : k + 1, :] for k in range(5)]

    mid = variant(ends, 0)
    mirror = list(mid)
    mirror[3] = -mirror[3]
    div_y = face_difference(variant(ends, 3), mid, variant(ends, 2), 1)
    div_z = face_difference(mirror, mid, variant(ends, 1), 2)
    for i in range(5):
        ends[2, i : i + 1, :] = div_y[i] + div_z[i]

    fetches["owner"].wait()
    fetches["target"].wait()
    owner_row = owner_ref[...].astype(f32)
    target_row = target_ref[...].astype(f32)
    row_id = lax.broadcasted_iota(jnp.int32, (blocks, blocks), 0)
    column_id = lax.broadcasted_iota(jnp.int32, (blocks, blocks), 1)
    diagonal = row_id == column_id
    owner = jnp.sum(jnp.where(diagonal, owner_row, 0.0), axis=1, keepdims=True)
    target = jnp.sum(jnp.where(diagonal, target_row, 0.0), axis=1, keepdims=True)
    same = jnp.where(owner == owner_row, 1.0, 0.0)
    rank = jnp.sum(jnp.where(column_id < row_id, same, 0.0), axis=1, keepdims=True)
    rank_row = jnp.sum(jnp.where(row_id < column_id, same, 0.0), axis=0, keepdims=True)
    lane_id = lax.broadcasted_iota(jnp.int32, (blocks, slot_count), 1).astype(f32)
    pick[...] = jnp.where(owner * capacity + rank == lane_id, 1.0, 0.0).astype(bf16)
    line_id = lax.broadcasted_iota(jnp.int32, (slot_count, blocks), 0).astype(f32)
    placed = jnp.where(owner_row * capacity + rank_row == line_id, 1.0, 0.0).astype(bf16)
    for part in range(3):
        place3[:, part * blocks : (part + 1) * blocks] = placed
    mine = (me * capacity).astype(f32)
    marks = jnp.where(mine + rank == lane_id, target + 1.0, 0.0).astype(bf16)
    peer_id = lax.broadcasted_iota(jnp.int32, (peers, blocks), 0).astype(f32)
    owned = jnp.where(peer_id == owner_row, 1.0, 0.0).astype(bf16)
    tags = jnp.dot(owned, marks, preferred_element_type=f32)
    for p in range(peers):
        note_out[p, :, 0:slot_count] = tags[p : p + 1, :]

    fetches["disp"].wait()
    pl.semaphore_wait(barrier, peers - 1)

    def near(slot, src, dst, distance):
        return pltpu.make_async_remote_copy(
            src_ref=src,
            dst_ref=dst,
            send_sem=near_send.at[slot],
            recv_sem=near_recv.at[slot],
            device_id=hop(distance),
            device_id_type=LOGICAL,
        )

    wall_up = near(0, ends.at[0], side_ref.at[0], 1)
    wall_down = near(1, ends.at[0], side_ref.at[1], peers - 1)
    prior = near(2, disp_ref.at[:, pl.ds(count - tail, tail), :], prior_ref, 1)
    bulks = []
    first_field = 0
    for slot, amount in enumerate((1, 2, 2)):
        part = pl.ds(first_field, amount)
        first_field += amount
        bulks.append(
            (
                near(3 + 2 * slot, prim.at[part], low_ref.at[part], 1),
                near(4 + 2 * slot, prim.at[part], high_ref.at[part], peers - 1),
            )
            if amount
            else ()
        )

    def spread(src, dst, sem, indexed):
        for step in steps:
            peer = hop(step)
            pltpu.make_async_remote_copy(
                src_ref=src.at[peer] if indexed else src,
                dst_ref=dst.at[me],
                send_sem=sem.at[0],
                recv_sem=sem.at[1],
                device_id=peer,
                device_id_type=LOGICAL,
            ).start()

    def gather(dst, sem):
        whole = dst.at[pl.ds(0, peers - 1)]
        return pltpu.make_async_remote_copy(
            src_ref=whole,
            dst_ref=whole,
            send_sem=sem.at[0],
            recv_sem=sem.at[1],
            device_id=hop(1),
            device_id_type=LOGICAL,
        )

    wall_up.start()
    wall_down.start()
    prior.start()

    fetches["res"].wait()
    for m in range(columns):
        for n in range(m, columns):
            line = jnp.sum(jnp.sum(res_ref[m] * res_ref[n], axis=0), axis=0, keepdims=True)
            lines[m * columns + n : m * columns + n + 1, :] = line
            lines[n * columns + m : n * columns + m + 1, :] = line

    def turn(value):
        kept = jnp.sum(value, axis=1, keepdims=True)
        shape = (value.shape[0], nodes)
        at = lax.broadcasted_iota(jnp.int32, shape, 0) == lax.broadcasted_iota(jnp.int32, shape, 1)
        return jnp.sum(jnp.where(at, kept, 0.0), axis=0, keepdims=True)

    gram_row = turn(lines[...])
    for p in range(peers):
        note_out[p, :, slot_count : slot_count + nodes] = gram_row
    spread(note_out, note_in, note_sem, True)
    for copy in bulks[0]:
        copy.start()
    note_in[me] = note_out[me]

    for c in range(3):
        held[pl.ds(8 + c, count, stride=8), :] = disp_ref[c]
    fetches["stiff"].wait()
    fetches["coup"].wait()

    def residual(t):
        both = jnp.concatenate([held[8 * t + 8 : 8 * t + 16, :], held[8 * t : 8 * t + 8, :]], axis=1)
        weights = jnp.concatenate([stiff_ref[t], coup_ref[t]], axis=1)
        solid[8 * t : 8 * t + 8, :] = lax.dot_general(
            both.astype(bf16), weights, LAST, preferred_element_type=f32
        )

    for t in range(1, count):
        residual(t)

    fetches["index"].wait()
    fetches["normals"].wait()
    fetches["rbf"].wait()
    wall_up.wait()
    wall_down.wait()

    div_x = face_difference(variant(side_ref, 0), mid, variant(side_ref, 1), 0)
    bottom = [
        row - step_ratio * (a + ends[2, i : i + 1, :])
        for i, (row, a) in enumerate(zip(conserve(mid), div_x))
    ]
    kinetic = bottom[1] * bottom[1] + bottom[2] * bottom[2] + bottom[3] * bottom[3]
    wall = (ratio_heat - 1.0) * (bottom[4] - 0.5 * kinetic / bottom[0])

    index = index_ref[...]
    low = index % nodes
    found = jnp.zeros(index.shape, f32)
    for part in range(wall.shape[1] // nodes):
        source = jnp.broadcast_to(wall[:, part * nodes : (part + 1) * nodes], index.shape)
        taken = jnp.take_along_axis(source, low, axis=1)
        found = jnp.where(index // nodes == part, taken, found)
    for c in range(3):
        lanes_in[pl.ds(c, blocks, stride=WIDE), :] = found * normals_ref[c]

    def pair(b):
        at = WIDE * b
        return jnp.concatenate(
            [lanes_in[at : at + 8, :], lanes_in[at + 8 : at + 16, :]], axis=1
        ).astype(bf16)

    for b in range(0, blocks, 2):
        weights = rbf_ref[b : b + 2].reshape(2 * nodes, nodes)
        lanes_out[4 * b : 4 * b + 8, :] = jnp.dot(pair(b), weights, preferred_element_type=f32)
    parts = [thirds(lanes_out[pl.ds(c, blocks, stride=4), :]) for c in range(3)]
    for c in range(3):
        stack = jnp.concatenate(parts[c], axis=0)
        placed = jnp.dot(place3[...], stack, preferred_element_type=f32)
        for p in range(peers):
            load_out[p, :, spans[c]] = placed[p * capacity : (p + 1) * capacity, :]
    spread(load_out, load_in, load_sem, True)
    for copy in bulks[1]:
        copy.start()
    load_in[me] = load_out[me]

    prior.wait()
    first = (me > 0).astype(f32)
    for c in range(3):
        held[c : c + 1, :] = prior_ref[c, tail - 1 : tail, :] * first
    residual(0)

    notes = gather(note_in, note_sem)
    notes.wait_recv()
    note = jnp.sum(note_in[...], axis=0)
    tag_row = note[:, 0:slot_count]
    marked = lax.broadcasted_iota(jnp.int32, (nodes, slot_count), 0).astype(f32) + 1.0 == tag_row
    marked = jnp.where(marked, 1.0, 0.0)
    collector = marked[0:count, :].astype(bf16)
    chooser = marked.T[:, 0:count].astype(bf16)
    shape = (columns, nodes)
    m_id = lax.broadcasted_iota(jnp.int32, shape, 0)
    n_id = lax.broadcasted_iota(jnp.int32, shape, 1)
    spot = jnp.minimum(m_id * columns + n_id, nodes - 1)
    gram = jnp.broadcast_to(note[:, slot_count : slot_count + nodes], shape)
    matrix = jnp.where(
        n_id < columns,
        jnp.take_along_axis(gram, spot, axis=1),
        jnp.where(n_id == m_id + columns, 1.0, 0.0),
    )
    for k in range(columns):
        line = matrix[k : k + 1, :]
        scaled = line / matrix[k : k + 1, k : k + 1]
        matrix = jnp.where(m_id == k, scaled, matrix - matrix[:, k : k + 1] * scaled)
    fetches["inv"].wait()
    fetches["dif"].wait()

    loads = gather(load_in, load_sem)
    loads.wait_recv()
    for p in range(peers):
        slots[p * capacity : (p + 1) * capacity, :] = load_in[p]
    high, middle, rest = thirds(slots[...])
    twice = jnp.concatenate([collector, collector], axis=1)
    served = jnp.dot(
        twice, jnp.concatenate([high, middle], axis=0), preferred_element_type=f32
    ) + jnp.dot(collector, rest, preferred_element_type=f32)
    change = [
        -inv_ref[c] * (solid[pl.ds(c, count, stride=8), :] - served[:, spans[c]])
        for c in range(3)
    ]
    for m in range(columns):
        line = sum(res_ref[m, c] * change[c] for c in range(3))
        lines[m : m + 1, :] = jnp.sum(line, axis=0, keepdims=True)
    share = sum(
        -matrix[:, columns + m : columns + m + 1] * lines[m : m + 1, :] for m in range(columns)
    )
    stat_out[...] = turn(share)
    spread(stat_out, stat_in, stat_sem, False)
    for copy in bulks[2]:
        copy.start()
    stat_in[me] = stat_out[...]
    base = [disp_ref[c] + change[c] for c in range(3)]
    stats = gather(stat_in, stat_sem)
    stats.wait_recv()
    mixing = jnp.broadcast_to(jnp.sum(stat_in[...], axis=0), (8, nodes))
    weights = [
        jnp.tile(jnp.broadcast_to(mixing[:, m : m + 1], (8, nodes)), (count // 8, 1))
        for m in range(columns)
    ]
    halves = []
    for c in range(3):
        result = base[c]
        for m in range(columns):
            result = result + dif_ref[m, c] * weights[m]
        next_ref[c] = result
        halves.append(result.astype(bf16))
    chosen = jnp.dot(chooser, jnp.concatenate(halves, axis=1), preferred_element_type=f32)
    for p in range(peers):
        reply_out[p] = chosen[p * capacity : (p + 1) * capacity, :].astype(bf16)
    spread(reply_out, reply_in, reply_sem, True)
    reply_in[me] = reply_out[me]

    for copy in bulks[0] + bulks[1] + bulks[2]:
        copy.wait()
    flow_section(fields, low_ref, high_ref, fluid_ref)

    replies = gather(reply_in, reply_sem)
    replies.wait_recv()
    for p in range(peers):
        slots[p * capacity : (p + 1) * capacity, :] = reply_in[p].astype(f32)
    rows = jnp.dot(pick[...], slots[...].astype(bf16), preferred_element_type=f32)
    for c in range(3):
        lanes_in[pl.ds(c, blocks, stride=WIDE), :] = rows[:, spans[c]]
    for b in range(0, blocks, 2):
        weights = jnp.concatenate([rbf_ref[b], rbf_ref[b + 1]], axis=1)
        lanes_out[4 * b : 4 * b + 8, :] = lax.dot_general(
            pair(b), weights, LAST, preferred_element_type=f32
        )
    for c in range(3):
        motion_ref[c] = lanes_out[pl.ds(c, blocks, stride=4), :]
    for copy in (notes, loads, stats, replies):
        copy.wait_send()


def finish_kernel(fluid_in, next_in, motion_in, fluid_ref, next_ref, motion_ref, sems):
    pairs = ((fluid_in, fluid_ref), (next_in, next_ref), (motion_in, motion_ref))
    copies = [pltpu.make_async_copy(a, b, sems.at[i]) for i, (a, b) in enumerate(pairs)]
    for copy in copies:
        copy.start()
    for copy in copies:
        copy.wait()


def rows_last(value):
    return jnp.swapaxes(value, -3, -2)


def on_device(
    density,
    velocity,
    pressure,
    rbf_blocks,
    correlation,
    normals,
    routes,
    targets,
    stiffness,
    coupling,
    inverse_diag,
    displacement,
    diff_res,
    diff_disp,
):
    f32, bf16, i32 = jnp.float32, jnp.bfloat16, jnp.int32
    width = lax.axis_size("dev")
    peers = lax.axis_size(AXES)
    blocks, nodes = correlation.shape
    count = displacement.shape[0]
    columns = diff_res.shape[0]
    height, depth = density.shape[1:]
    capacity = max(2, 2 * blocks // peers)
    slot_count = peers * capacity
    row = 3 * nodes

    padded = -(-height // depth) * depth
    halo = (5, height, depth)
    vmem = pl.BlockSpec(memory_space=pltpu.VMEM)
    hbm = pl.BlockSpec(memory_space=pltpu.HBM)
    anywhere = pl.BlockSpec(memory_space=pl.ANY)
    dma = pltpu.SemaphoreType.DMA
    shapes = (
        jax.ShapeDtypeStruct((5,) + density.shape, f32),
        jax.ShapeDtypeStruct((3, count, nodes), f32),
        jax.ShapeDtypeStruct((3, blocks, nodes), f32),
    )
    operands = (
        density,
        velocity,
        pressure,
        routes.reshape(1, blocks),
        targets.reshape(1, blocks),
        rows_last(diff_res),
        rows_last(displacement),
        correlation,
        rows_last(normals),
        rbf_blocks,
        stiffness,
        coupling,
        rows_last(inverse_diag),
        rows_last(diff_disp),
    )
    operands = [pltpu.with_memory_space_constraint(x, pltpu.HBM) for x in operands]
    outputs = pl.pallas_call(
        functools.partial(couple_kernel, peers, width),
        out_shape=shapes,
        in_specs=[hbm] * len(operands),
        out_specs=(vmem, vmem, vmem),
        scratch_shapes=[pltpu.VMEM(x.shape, x.dtype) for x in operands]
        + [
            pltpu.VMEM((4, 8, padded), f32),
            pltpu.VMEM(halo, bf16),
            pltpu.VMEM(halo, bf16),
            pltpu.VMEM(halo, bf16),
            pltpu.VMEM((2, 8, padded), f32),
            pltpu.VMEM((3, 8, nodes), f32),
            pltpu.VMEM((peers, 1, slot_count + nodes), f32),
            pltpu.VMEM((peers, 1, slot_count + nodes), f32),
            pltpu.VMEM((peers, capacity, row), f32),
            pltpu.VMEM((peers, capacity, row), f32),
            pltpu.VMEM((peers, capacity, row), bf16),
            pltpu.VMEM((peers, capacity, row), bf16),
            pltpu.VMEM((1, nodes), f32),
            pltpu.VMEM((peers, 1, nodes), f32),
            pltpu.VMEM((blocks, slot_count), bf16),
            pltpu.VMEM((slot_count, 3 * blocks), bf16),
            pltpu.VMEM((blocks * WIDE, nodes), f32),
            pltpu.VMEM((blocks * 4, nodes), f32),
            pltpu.VMEM((slot_count, row), f32),
            pltpu.VMEM((count * 8 + 8, nodes), f32),
            pltpu.VMEM((count * 8, nodes), f32),
            pltpu.VMEM((columns * columns, nodes), f32),
            dma((len(operands),)),
            dma((9,)),
            dma((9,)),
            dma((2,)),
            dma((2,)),
            dma((2,)),
            dma((2,)),
        ],
        compiler_params=pltpu.CompilerParams(
            collective_id=0, has_side_effects=True, vmem_limit_bytes=24 * 2**20
        ),
    )(*operands)
    fluid_next, disp_next, wall_motion = pl.pallas_call(
        finish_kernel,
        out_shape=shapes,
        in_specs=[vmem] * 3,
        out_specs=(anywhere,) * 3,
        scratch_shapes=[dma((3,))],
        compiler_params=pltpu.CompilerParams(vmem_limit_bytes=16 * 2**20),
    )(*outputs)
    return (fluid_next, rows_last(disp_next), rows_last(wall_motion))


def solution(mesh):
    placed = (
        P(("group", "dev"), None, None),
        P(None, ("group", "dev"), None, None),
        P(("group", "dev"), None, None),
        P(("group", "dev"), None, None),
        P(("group", "dev"), None),
        P(("group", "dev"), None, None),
        P(("group", "dev"), None),
        P(("group", "dev")),
        P(("group", "dev"), None, None),
        P(("group", "dev"), None, None),
        P(("group", "dev"), None, None),
        P(("group", "dev"), None, None),
        P(None, ("group", "dev"), None, None),
        P(None, ("group", "dev"), None, None),
    )
    return jax.shard_map(
        on_device,
        mesh=mesh,
        in_specs=placed,
        out_specs=(
            P(None, ("group", "dev"), None, None),
            P(("group", "dev"), None, None),
            P(("group", "dev"), None, None),
        ),
        check_vma=False,
    )
```
